32 devices in a mesh: row: 2 (over y), col: 4 (over z), layer: 4 (over x, core).
Axes of the slice: x: 2, y: 2, z: 4, core: 2. Of those that a mesh axis runs over, the one named last changes fastest.
Arguments:
- density: bfloat16 [128, 4, 128, 128], P(('row', 'col')), may hold values from -1.1953125 to 1.1953125
- tile_cols: int32 [128, 4], replicated, may hold values from 0 to 127, as said below
- out_cols: int32 [128, 4, 4], P(('row', 'col')), may hold values from 0 to 127, as said below
Outputs:
- purified: bfloat16 [128, 4, 4, 128, 128], P(('row', 'col'), 'layer')
The draws below stay inside these ranges and needn't reach their ends.
Inputs may be any that keep to these rules, and one draw needn't show every extreme that they name: Column set l holds the block columns c with (c // 4) % 4 == l; tile_cols[i, l] lies in column set l, so a block row has exactly one tile in each column set. For each i and l, the 4 block columns out_cols[i, l, :] are distinct and lie in column set l.
All inputs are finite; a program needn't handle non-finite values.
Results may differ from the reference program's by a relative error of at most 0.0044.
Values may be sent and summed in bfloat16 or wider, within the bound.
A program may use at most 128 MiB of HBM per device.

```python
import jax
import jax.numpy as jnp
from jax import lax

BS = 128
GROUP_ROWS = 16
KQ = 4
LAYERS = 4
GROUPS = 8
SUB_ROWS = 4
NB = 128


def settle(candidate, earlier):
    shifts = [(candidate + j * GROUP_ROWS) % NB for j in range(KQ)]
    stacked = jnp.stack(shifts, axis=-1)
    if earlier:
        unused = jnp.stack([jnp.all(jnp.stack([shifted != before for before in earlier], axis=0), axis=0) for shifted in shifts], axis=-1)
    else:
        unused = jnp.ones(stacked.shape, dtype=bool)
    chosen_shift = jnp.argmax(unused.astype(jnp.int32), axis=-1)
    return jnp.take_along_axis(stacked, chosen_shift[..., None], axis=-1)[..., 0]


def pattern(key):
    groups_drawn = jax.random.randint(jax.random.fold_in(key, 101), (NB, LAYERS), 0, GROUPS)
    within = jax.random.randint(jax.random.fold_in(key, 202), (NB, LAYERS), 0, SUB_ROWS)
    set_ids = jnp.arange(LAYERS, dtype=jnp.int32)[None, :]
    tile_cols = (groups_drawn * GROUP_ROWS + set_ids * SUB_ROWS + within).astype(jnp.int32)
    set_grid = jnp.arange(LAYERS, dtype=jnp.int32)[None, :, None]
    slot_draw = jax.random.randint(jax.random.fold_in(key, 303), (NB, LAYERS * 2), 0, LAYERS)
    through = jnp.take_along_axis(tile_cols, slot_draw, axis=1).reshape(NB, LAYERS, 2)
    reach_one = tile_cols[through, set_grid]
    slot_zero = settle(reach_one[:, :, 0], [])
    slot_one = settle(reach_one[:, :, 1], [slot_zero])
    base = jnp.stack([slot_zero, slot_one], axis=-1).reshape(NB, LAYERS * 2)
    via_draw = jax.random.randint(jax.random.fold_in(key, 404), (NB, LAYERS * 2), 0, LAYERS * 2)
    through_two = jnp.take_along_axis(base, via_draw, axis=1).reshape(NB, LAYERS, 2)
    reach_two = tile_cols[through_two, set_grid]
    slot_two = settle(reach_two[:, :, 0], [slot_zero, slot_one])
    slot_three = settle(reach_two[:, :, 1], [slot_zero, slot_one, slot_two])
    out_cols = jnp.stack([slot_zero, slot_one, slot_two, slot_three], axis=-1).astype(jnp.int32)
    return (tile_cols, out_cols)


def draw_tile_cols(key, part):
    return pattern(key)[0]


def draw_out_cols(key, part):
    return pattern(key)[1]


def steps_of(key, dims, split, low, top_value):
    factor_of = 1.0
    for axis_at, parts in split:
        heights = jax.random.uniform(jax.random.fold_in(jax.random.fold_in(key, 6), axis_at), (parts,), jnp.float32, low / len(split), top_value / len(split))
        factor_of = factor_of * jnp.repeat(jnp.exp(heights), dims[axis_at] // parts).reshape((-1,) + (1,) * (len(dims) - 1 - axis_at))
    return factor_of


def gaussian(stream_key, dims, width, most, cuts=(), kind=jnp.bfloat16):
    entries = jax.random.normal(stream_key, dims, jnp.float32) * width
    if len(cuts) > 0:
        entries = steps_of(stream_key, dims, cuts, -0.22, 0.18) * entries
    return jnp.clip(entries, min=-most, max=most).astype(kind)


def setup_inputs(seed: int = 0) -> dict:
    streams_of = jax.random.split(jax.random.key(seed), 4)
    density = gaussian(streams_of[0], (NB, LAYERS, BS, BS), 0.2, 1.1953125, ((0, 8),))
    tile_cols = draw_tile_cols(jax.random.fold_in(streams_of[3], 71), 0)
    out_cols = draw_out_cols(jax.random.fold_in(streams_of[3], 71), 0)
    return {"density": density, "tile_cols": tile_cols, "out_cols": out_cols}


def filtered_product(left_tiles, index_tiles, column, colset, wanted):
    step_rows = 32

    def row_block(first_row):
        left_part = lax.dynamic_slice_in_dim(left_tiles, first_row, step_rows, 0).astype(jnp.float32)
        index_part = lax.dynamic_slice_in_dim(index_tiles, first_row, step_rows, 0)
        wanted_part = lax.dynamic_slice_in_dim(wanted, first_row, step_rows, 0)
        b_tiles = jnp.take(column, index_part, axis=0).astype(jnp.float32)
        products = jnp.einsum("imab,imbc->imac", left_part, b_tiles, precision=lax.Precision.HIGHEST)
        matches = (jnp.take(colset, index_part, axis=0)[:, :, None] == wanted_part[:, None, :]).astype(jnp.float32)
        return jnp.einsum("imq,imac->iqac", matches, products, precision=lax.Precision.HIGHEST)

    starts = jnp.arange(left_tiles.shape[0] // step_rows, dtype=jnp.int32) * step_rows
    blocks = lax.map(row_block, starts)
    return blocks.reshape((left_tiles.shape[0],) + blocks.shape[2:])


def reference(density, tile_cols, out_cols):
    layer_ids = jnp.arange(LAYERS, dtype=jnp.int32)

    def square_set(layer_id):
        column = lax.dynamic_index_in_dim(density, layer_id, 1, keepdims=False)
        colset = lax.dynamic_index_in_dim(tile_cols, layer_id, 1, keepdims=False)
        wanted = lax.dynamic_index_in_dim(out_cols, layer_id, 1, keepdims=False)
        return filtered_product(density, tile_cols, column, colset, wanted)

    square = jnp.moveaxis(lax.map(square_set, layer_ids), 0, 1)
    square_low = square.astype(jnp.bfloat16).reshape(NB, LAYERS * KQ, BS, BS)
    cube_index = out_cols.reshape(NB, LAYERS * KQ)

    def purify_set(layer_id):
        column = lax.dynamic_index_in_dim(density, layer_id, 1, keepdims=False)
        colset = lax.dynamic_index_in_dim(tile_cols, layer_id, 1, keepdims=False)
        wanted = lax.dynamic_index_in_dim(out_cols, layer_id, 1, keepdims=False)
        cube = filtered_product(square_low, cube_index, column, colset, wanted)
        own_square = lax.dynamic_index_in_dim(square, layer_id, 1, keepdims=False)
        return (3.0 * own_square - 2.0 * cube).astype(jnp.bfloat16)

    return jnp.moveaxis(lax.map(purify_set, layer_ids), 0, 1)
```

```python
import functools

import jax
import jax.numpy as jnp
from jax import lax
from jax.experimental import pallas as pl
from jax.experimental.pallas import tpu as pltpu
from jax.sharding import PartitionSpec as P

MESH = pl.DeviceIdType.MESH


def chunk_plan(own):
    early = max(own // 8, 1)
    half = (own - early) // 2
    return ((0, early), (early, half), (early + half, own - early - half))


def purify_kernel(
    R, C, L, den_hbm, tc, oc, out_hbm, col, den, square, low, result,
    den_sem, out_sem, recv, right_sem, left_sem, far_right, far_left, row_sem,
    recv_low, send_low, relay_low,
):
    own = den_hbm.shape[0]
    bs = den_hbm.shape[2]
    kq = oc.shape[2]
    plan = chunk_plan(own)
    r, c, l = lax.axis_index("row"), lax.axis_index("col"), lax.axis_index("layer")
    g = r * C + c
    partner = l + 1 - 2 * lax.rem(l, 2)
    rows = [lax.rem(r + d, R) for d in range(1, R)]
    twins = [lax.rem(l + 2 * d, L) for d in range(1, L // 2)]

    own_copy = pltpu.make_async_copy(den_hbm.at[:, l], col.at[pl.ds(g * own, own)], den_sem.at[0])
    own_copy.start()
    den_copy = pltpu.make_async_copy(den_hbm, den, den_sem.at[1])
    den_copy.start()

    barrier = pltpu.get_barrier_semaphore()

    def greet(**where):
        pl.semaphore_signal(barrier, inc=1, device_id=where, device_id_type=MESH)

    for other in rows:
        greet(row=other)
    for other in twins + [partner]:
        greet(layer=other)

    @pl.when(c > 0)
    def _():
        greet(col=c - 1)

    @pl.when(c < C - 1)
    def _():
        greet(col=c + 1)

    inner = jnp.where(c > 0, 1, 0) + jnp.where(c < C - 1, 1, 0)
    pl.semaphore_wait(barrier, (R - 1) + (L // 2) + inner)

    def tiles(group, ch):
        return col.at[pl.ds(group * own + plan[ch][0], plan[ch][1])]

    def move(group, ch, sem, where):
        return pltpu.make_async_remote_copy(
            src_ref=tiles(group, ch),
            dst_ref=tiles(group, ch),
            send_sem=sem,
            recv_sem=recv.at[group, ch],
            device_id=where,
            device_id_type=MESH,
        )

    def arrived(group, ch):
        move(group, ch, den_sem.at[0], {"layer": partner}).wait_recv()

    def to_right(group, ch, sem, act, step=0):
        @pl.when(jnp.minimum(c - step, C - 2 - c) >= 0)
        def _():
            act(move(group, ch, sem, {"col": c + 1}))

    def to_left(group, ch, sem, act, step=0):
        @pl.when(jnp.minimum(C - 1 - step - c, c - 1) >= 0)
        def _():
            act(move(group, ch, sem, {"col": c - 1}))

    def to_rows(group, ch, at, act):
        for d, other in enumerate(rows):
            act(move(group, ch, row_sem.at[d, at, ch], {"row": other}))

    def go(copy):
        copy.start()

    def done(copy):
        copy.wait_send()

    own_copy.wait()
    to_rows(g, 0, c, go)
    for ch in (1, 2, 0):
        to_right(g, ch, right_sem.at[c, ch], go)
        to_left(g, ch, left_sem.at[c, ch], go)
        if ch > 0:
            to_rows(g, ch, c, go)
    for d, other in enumerate(rows):
        group = other * C + c
        arrived(group, 0)
        to_right(group, 0, far_right.at[d, c], go)
        to_left(group, 0, far_left.at[d, c], go)

    def line(step, arrive):
        act = go if arrive else done
        before = jnp.maximum(c - step, 0)
        after = jnp.minimum(c + step, C - 1)
        for ch in (1, 2, 0):
            @pl.when(c >= step)
            def _():
                if arrive:
                    arrived(r * C + before, ch)
                if ch > 0:
                    to_rows(r * C + before, ch, before, act)

            to_right(r * C + before, ch, right_sem.at[before, ch], act, step)

            @pl.when(c + step < C)
            def _():
                if arrive:
                    arrived(r * C + after, ch)
                if ch > 0:
                    to_rows(r * C + after, ch, after, act)

            to_left(r * C + after, ch, left_sem.at[after, ch], act, step)
        for d, other in enumerate(rows):
            if arrive:
                @pl.when(c >= step)
                def _():
                    arrived(other * C + before, 0)
            to_right(other * C + before, 0, far_right.at[d, before], act, step)
            if arrive:
                @pl.when(c + step < C)
                def _():
                    arrived(other * C + after, 0)
            to_left(other * C + after, 0, far_left.at[d, after], act, step)

    for step in range(1, C):
        line(step, True)
    den_copy.wait()
    for at in range(C):
        for other in rows:
            for ch in (1, 2):
                arrived(other * C + at, ch)

    def masked(ks, wanted):
        columns = [[] for _ in range(kq)]
        for k in ks:
            tile = col[k]
            reached = tc[k, l]
            for q in range(kq):
                columns[q].append(lax.select(reached == wanted[q], tile, jnp.zeros_like(tile)))
        return jnp.concatenate([jnp.concatenate(parts, axis=0) for parts in columns], axis=1)

    def low_move(u, i, sem, where):
        return pltpu.make_async_remote_copy(
            src_ref=low.at[u, i],
            dst_ref=low.at[u, i],
            send_sem=sem,
            recv_sem=recv_low.at[u, i],
            device_id={"layer": where},
            device_id_type=MESH,
        )

    def low_arrived(u, i):
        low_move(u, i, den_sem.at[0], partner).wait_recv()

    def send_row(i, act):
        for d, other in enumerate(twins + [partner]):
            act(low_move(l, i, send_low.at[d, i], other))

    def square_row(i, carry):
        wanted = [oc[i, l, q] for q in range(kq)]
        left = jnp.concatenate([den[i, s] for s in range(L)], axis=1)
        right = masked([tc[g * own + i, s] for s in range(L)], wanted)
        total = jnp.dot(left, right, preferred_element_type=jnp.float32)
        square[i] = total
        low[l, i] = total.astype(jnp.bfloat16)

        @pl.when(i > 0)
        def _():
            send_row(i - 1, go)

        return carry

    lax.fori_loop(0, own, square_row, 0)
    send_row(own - 1, go)

    def relay(i, act):
        for d, other in enumerate(twins):
            if act is go:
                low_arrived(other, i)
            act(low_move(other, i, relay_low.at[d, i], partner))

    def cube_row(i):
        low_arrived(partner, i)
        for other in twins:
            low_arrived(other + 1 - 2 * lax.rem(other, 2), i)
        wanted = [oc[i, l, q] for q in range(kq)]
        total = jnp.zeros((bs, kq * bs), jnp.float32)
        for u in range(L):
            right = masked([oc[i, u, t] for t in range(kq)], wanted)
            total += jnp.dot(low[u, i], right, preferred_element_type=jnp.float32)
        value = (3.0 * square[i] - 2.0 * total).astype(jnp.bfloat16)
        for q in range(kq):
            result[i, q] = value[:, q * bs:(q + 1) * bs]

    def write(i):
        return pltpu.make_async_copy(result.at[i], out_hbm.at[i, 0], out_sem.at[i])

    relay(0, go)

    def cube_step(i, carry):
        relay(i, go)
        cube_row(i - 1)

        @pl.when(i > 1)
        def _():
            write(i - 2).start()

        return carry

    lax.fori_loop(1, own, cube_step, 0)
    cube_row(own - 1)
    if own > 1:
        write(own - 2).start()
    write(own - 1).start()

    to_rows(g, 0, c, done)
    for ch in (1, 2, 0):
        to_right(g, ch, right_sem.at[c, ch], done)
        to_left(g, ch, left_sem.at[c, ch], done)
        if ch > 0:
            to_rows(g, ch, c, done)
    for d, other in enumerate(rows):
        to_right(other * C + c, 0, far_right.at[d, c], done)
        to_left(other * C + c, 0, far_left.at[d, c], done)
    for step in range(1, C):
        line(step, False)

    def finish(i, carry):
        send_row(i, done)
        relay(i, done)
        write(i).wait()
        return carry

    lax.fori_loop(0, own, finish, 0)


def on_device(R, C, L, density, tile_cols, out_cols):
    own, _, bs, _ = density.shape
    kq = out_cols.shape[2]
    groups = R * C
    dma = pltpu.SemaphoreType.DMA
    bf16, f32 = jnp.bfloat16, jnp.float32
    return pl.pallas_call(
        functools.partial(purify_kernel, R, C, L),
        out_shape=jax.ShapeDtypeStruct((own, 1, kq, bs, bs), bf16),
        in_specs=[
            pl.BlockSpec(memory_space=pl.ANY),
            pl.BlockSpec(memory_space=pltpu.SMEM),
            pl.BlockSpec(memory_space=pltpu.SMEM),
        ],
        out_specs=pl.BlockSpec(memory_space=pl.ANY),
        scratch_shapes=[
            pltpu.VMEM((groups * own, bs, bs), bf16),
            pltpu.VMEM((own, L, bs, bs), bf16),
            pltpu.VMEM((own, bs, kq * bs), f32),
            pltpu.VMEM((L, own, bs, kq * bs), bf16),
            pltpu.VMEM((own, kq, bs, bs), bf16),
            dma((2,)),
            dma((own,)),
            dma((groups, 3)),
            dma((C, 3)),
            dma((C, 3)),
            dma((max(R - 1, 1), C)),
            dma((max(R - 1, 1), C)),
            dma((max(R - 1, 1), C, 3)),
            dma((L, own)),
            dma((L // 2, own)),
            dma((max(L // 2 - 1, 1), own)),
        ],
        compiler_params=pltpu.CompilerParams(
            collective_id=0, has_side_effects=True, vmem_limit_bytes=60 * 2**20
        ),
    )(density, tile_cols, out_cols)


def solution(mesh):
    R, C, L = (mesh.shape[name] for name in ("row", "col", "layer"))
    placed = (P(("row", "col"), None, None, None), P(), P(("row", "col"), None, None))
    return jax.shard_map(
        functools.partial(on_device, R, C, L),
        mesh=mesh,
        in_specs=placed,
        out_specs=P(("row", "col"), "layer", None, None, None),
        check_vma=False,
    )
```

```python
import functools

import jax
import jax.numpy as jnp
from jax import lax
from jax.experimental import pallas as pl
from jax.experimental.pallas import tpu as pltpu
from jax.sharding import PartitionSpec as P

MESH = pl.DeviceIdType.MESH


def chunk_plan(own):
    early = max(own // 8, 1)
    plan, start = [(0, early)], early
    for left in range(4, 0, -1):
        size = (own - start + left - 1) // left
        if size > 0:
            plan.append((start, size))
        start += size
    return plan


def purify_kernel(
    R, C, L, paired, den_hbm, tc, oc, out_hbm, col, den, square, low, result,
    den_sem, out_sem, recv, right_sem, left_sem, far_right, far_left, row_sem,
    recv_low, send_low, relay_low, extra, twin_recv, twin_sem,
):
    own = den_hbm.shape[0]
    bs = den_hbm.shape[2]
    kq = oc.shape[2]
    plan = chunk_plan(own)
    r, c, l = lax.axis_index("row"), lax.axis_index("col"), lax.axis_index("layer")
    g = r * C + c
    partner = l + 1 - 2 * lax.rem(l, 2)
    rows = [lax.rem(r + d, R) for d in range(1, R)]
    odd = lax.rem(l, 2)
    late = range(1, len(plan))
    order = [*late, 0]
    if paired:
        pair, half = l // 4, lax.rem(l // 2, 2)
        twin = l + 2 - 4 * half
        twins = [twin]
        for e in range(1, L // 4):
            first = 4 * lax.rem(pair + e, L // 4) + odd
            twins += [first, first + 2]
    else:
        twins = [lax.rem(l + 2 * d, L) for d in range(1, L // 2)]

    own_copy = pltpu.make_async_copy(den_hbm.at[:, l], col.at[pl.ds(g * own, own)], den_sem.at[0])
    own_copy.start()
    den_copy = pltpu.make_async_copy(den_hbm, den, den_sem.at[1])
    den_copy.start()
    if paired:
        twin_copy = pltpu.make_async_copy(
            den_hbm.at[:, twin], extra.at[pl.ds(g * own, own)], den_sem.at[2]
        )
        twin_copy.start()

    barrier = pltpu.get_barrier_semaphore()

    def greet(**where):
        pl.semaphore_signal(barrier, inc=1, device_id=where, device_id_type=MESH)

    for other in rows:
        greet(row=other)
    for other in twins + [partner]:
        greet(layer=other)

    @pl.when(c > 0)
    def _():
        greet(col=c - 1)

    @pl.when(c < C - 1)
    def _():
        greet(col=c + 1)

    inner = jnp.where(c > 0, 1, 0) + jnp.where(c < C - 1, 1, 0)
    pl.semaphore_wait(barrier, (R - 1) + (L // 2) + inner)

    def tiles(group, ch):
        return col.at[pl.ds(group * own + plan[ch][0], plan[ch][1])]

    def move(group, ch, sem, where):
        return pltpu.make_async_remote_copy(
            src_ref=tiles(group, ch),
            dst_ref=tiles(group, ch),
            send_sem=sem,
            recv_sem=recv.at[group, ch],
            device_id=where,
            device_id_type=MESH,
        )

    def arrived(group, ch):
        move(group, ch, den_sem.at[0], {"layer": partner}).wait_recv()

    def to_right(group, ch, sem, act, step=0):
        @pl.when(jnp.minimum(c - step, C - 2 - c) >= 0)
        def _():
            act(move(group, ch, sem, {"col": c + 1}))

    def to_left(group, ch, sem, act, step=0):
        @pl.when(jnp.minimum(C - 1 - step - c, c - 1) >= 0)
        def _():
            act(move(group, ch, sem, {"col": c - 1}))

    def to_rows(group, ch, at, act):
        for d, other in enumerate(rows):
            act(move(group, ch, row_sem.at[d, at, ch], {"row": other}))

    def twin_move(group, ch):
        part = pl.ds(group * own + plan[ch][0], plan[ch][1])
        return pltpu.make_async_remote_copy(
            src_ref=col.at[part],
            dst_ref=extra.at[part],
            send_sem=twin_sem.at[group, ch],
            recv_sem=twin_recv.at[group, ch],
            device_id={"layer": twin},
            device_id_type=MESH,
        )

    def to_twin(group, ch, ok):
        if paired:
            @pl.when(jnp.minimum(ok, -odd) >= 0)
            def _():
                twin_move(group, ch).start()

    def go(copy):
        copy.start()

    def done(copy):
        copy.wait_send()

    own_copy.wait()
    to_rows(g, 0, c, go)
    for ch in order:
        to_right(g, ch, right_sem.at[c, ch], go)
        to_left(g, ch, left_sem.at[c, ch], go)
        if ch > 0:
            to_rows(g, ch, c, go)
    for d, other in enumerate(rows):
        group = other * C + c
        arrived(group, 0)
        to_twin(group, 0, 0)
        to_right(group, 0, far_right.at[d, c], go)
        to_left(group, 0, far_left.at[d, c], go)

    def line(step, arrive):
        act = go if arrive else done
        before = jnp.maximum(c - step, 0)
        after = jnp.minimum(c + step, C - 1)
        for ch in order:
            @pl.when(c >= step)
            def _():
                if arrive:
                    arrived(r * C + before, ch)
                if ch > 0:
                    to_rows(r * C + before, ch, before, act)

            to_right(r * C + before, ch, right_sem.at[before, ch], act, step)
            if arrive:
                to_twin(r * C + before, ch, c - step)

            @pl.when(c + step < C)
            def _():
                if arrive:
                    arrived(r * C + after, ch)
                if ch > 0:
                    to_rows(r * C + after, ch, after, act)

            to_left(r * C + after, ch, left_sem.at[after, ch], act, step)
            if arrive:
                to_twin(r * C + after, ch, C - 1 - step - c)
        for d, other in enumerate(rows):
            if arrive:
                @pl.when(c >= step)
                def _():
                    arrived(other * C + before, 0)
            to_right(other * C + before, 0, far_right.at[d, before], act, step)
            if arrive:
                to_twin(other * C + before, 0, c - step)
            if arrive:
                @pl.when(c + step < C)
                def _():
                    arrived(other * C + after, 0)
            to_left(other * C + after, 0, far_left.at[d, after], act, step)
            if arrive:
                to_twin(other * C + after, 0, C - 1 - step - c)

    def crossed(step):
        before = jnp.maximum(c - step, 0)
        after = jnp.minimum(c + step, C - 1)
        for other in rows:
            for ch in late:
                @pl.when(c >= step)
                def _():
                    arrived(other * C + before, ch)

                to_twin(other * C + before, ch, c - step)
                if step > 0:
                    @pl.when(c + step < C)
                    def _():
                        arrived(other * C + after, ch)

                    to_twin(other * C + after, ch, C - 1 - step - c)

    for step in range(1, C):
        line(step, True)
        crossed(step - 1)
    crossed(C - 1)
    den_copy.wait()

    def masked(ks, wanted, source, layer):
        columns = [[] for _ in range(kq)]
        for k in ks:
            tile = source[k]
            reached = tc[k, layer]
            for q in range(kq):
                columns[q].append(lax.select(reached == wanted[q], tile, jnp.zeros_like(tile)))
        return jnp.concatenate([jnp.concatenate(parts, axis=0) for parts in columns], axis=1)

    def low_move(u, i, sem, where):
        return pltpu.make_async_remote_copy(
            src_ref=low.at[u, i],
            dst_ref=low.at[u, i],
            send_sem=sem,
            recv_sem=recv_low.at[u, i],
            device_id={"layer": where},
            device_id_type=MESH,
        )

    def low_arrived(u, i):
        low_move(u, i, den_sem.at[0], partner).wait_recv()

    def send_row(i, act):
        for d, other in enumerate(twins + [partner]):
            if paired and d == 0:
                @pl.when(odd == 1)
                def _():
                    act(low_move(l, i, send_low.at[0, i], twins[0]))
            else:
                act(low_move(l, i, send_low.at[d, i], other))

    def square_row(i, source, layer):
        wanted = [oc[i, layer, q] for q in range(kq)]
        left = jnp.concatenate([den[i, s] for s in range(L)], axis=1)
        right = masked([tc[g * own + i, s] for s in range(L)], wanted, source, layer)
        total = jnp.dot(left, right, preferred_element_type=jnp.float32)
        low[layer, i] = total.astype(jnp.bfloat16)
        return total

    def own_row(i):
        square[i] = square_row(i, col, l)

    def own_step(i, carry):
        own_row(i)
        send_row(i - 1, go)
        return carry

    own_row(0)
    lax.fori_loop(1, own, own_step, 0)
    send_row(own - 1, go)

    if paired:
        twin_copy.wait()

        @pl.when(odd == 0)
        def _():
            for j in range(1, R * C):
                for ch in order:
                    twin_move(lax.rem(g + j, R * C), ch).wait_recv()

            def pass_on(i):
                low_move(twin, i, relay_low.at[0, i], partner).start()

            def twin_step(i, carry):
                square_row(i, extra, twin)
                pass_on(i - 1)
                return carry

            square_row(0, extra, twin)
            lax.fori_loop(1, own, twin_step, 0)
            pass_on(own - 1)

    def relay(i, act):
        for d, other in enumerate(twins):
            if paired and d == 0 and act is go:
                @pl.when(odd == 1)
                def _():
                    low_arrived(twin, i)
                    low_move(twin, i, relay_low.at[0, i], partner).start()
                continue
            if act is go:
                low_arrived(other, i)
            act(low_move(other, i, relay_low.at[d, i], partner))

    def cube_row(i):
        low_arrived(partner, i)
        for other in twins:
            low_arrived(other + 1 - 2 * lax.rem(other, 2), i)
        wanted = [oc[i, l, q] for q in range(kq)]
        total = jnp.zeros((bs, kq * bs), jnp.float32)
        for u in range(L):
            right = masked([oc[i, u, t] for t in range(kq)], wanted, col, l)
            total += jnp.dot(low[u, i], right, preferred_element_type=jnp.float32)
        value = (3.0 * square[i] - 2.0 * total).astype(jnp.bfloat16)
        for q in range(kq):
            result[i, q] = value[:, q * bs:(q + 1) * bs]

    def write(i):
        return pltpu.make_async_copy(result.at[i], out_hbm.at[i, 0], out_sem.at[i])

    relay(0, go)

    def cube_step(i, carry):
        relay(i, go)
        cube_row(i - 1)

        @pl.when(i > 1)
        def _():
            write(i - 2).start()

        return carry

    lax.fori_loop(1, own, cube_step, 0)
    cube_row(own - 1)
    if own > 1:
        write(own - 2).start()
    write(own - 1).start()

    to_rows(g, 0, c, done)
    for ch in order:
        to_right(g, ch, right_sem.at[c, ch], done)
        to_left(g, ch, left_sem.at[c, ch], done)
        if ch > 0:
            to_rows(g, ch, c, done)
    for d, other in enumerate(rows):
        to_right(other * C + c, 0, far_right.at[d, c], done)
        to_left(other * C + c, 0, far_left.at[d, c], done)
    for step in range(1, C):
        line(step, False)

    if paired:
        @pl.when(odd == 0)
        def _():
            for j in range(1, R * C):
                for ch in order:
                    twin_move(lax.rem(g + j, R * C), ch).wait_send()

    def finish(i, carry):
        send_row(i, done)
        relay(i, done)
        write(i).wait()
        return carry

    lax.fori_loop(0, own, finish, 0)


def on_device(R, C, L, density, tile_cols, out_cols):
    own, _, bs, _ = density.shape
    kq = out_cols.shape[2]
    groups = R * C
    parts = len(chunk_plan(own))
    paired = L % 4 == 0
    dma = pltpu.SemaphoreType.DMA
    bf16, f32 = jnp.bfloat16, jnp.float32
    return pl.pallas_call(
        functools.partial(purify_kernel, R, C, L, paired),
        out_shape=jax.ShapeDtypeStruct((own, 1, kq, bs, bs), bf16),
        in_specs=[
            pl.BlockSpec(memory_space=pl.ANY),
            pl.BlockSpec(memory_space=pltpu.SMEM),
            pl.BlockSpec(memory_space=pltpu.SMEM),
        ],
        out_specs=pl.BlockSpec(memory_space=pl.ANY),
        scratch_shapes=[
            pltpu.VMEM((groups * own, bs, bs), bf16),
            pltpu.VMEM((own, L, bs, bs), bf16),
            pltpu.VMEM((own, bs, kq * bs), f32),
            pltpu.VMEM((L, own, bs, kq * bs), bf16),
            pltpu.VMEM((own, kq, bs, bs), bf16),
            dma((3,)),
            dma((own,)),
            dma((groups, parts)),
            dma((C, parts)),
            dma((C, parts)),
            dma((max(R - 1, 1), C)),
            dma((max(R - 1, 1), C)),
            dma((max(R - 1, 1), C, parts)),
            dma((L, own)),
            dma((L // 2, own)),
            dma((max(L // 2 - 1, 1), own)),
            pltpu.VMEM((groups * own if paired else 1, bs, bs), bf16),
            dma((groups, parts)),
            dma((groups, parts)),
        ],
        compiler_params=pltpu.CompilerParams(
            collective_id=0, has_side_effects=True, vmem_limit_bytes=60 * 2**20
        ),
    )(density, tile_cols, out_cols)


def solution(mesh):
    R, C, L = (mesh.shape[name] for name in ("row", "col", "layer"))
    placed = (P(("row", "col"), None, None, None), P(), P(("row", "col"), None, None))
    return jax.shard_map(
        functools.partial(on_device, R, C, L),
        mesh=mesh,
        in_specs=placed,
        out_specs=P(("row", "col"), "layer", None, None, None),
        check_vma=False,
    )
```

```python
import functools

import jax
import jax.numpy as jnp
from jax import lax
from jax.experimental import pallas as pl
from jax.experimental.pallas import tpu as pltpu
from jax.sharding import PartitionSpec as P

MESH = pl.DeviceIdType.MESH


def chunk_plan(own):
    early = max(own // 8, 1)
    plan, start = [(0, early)], early
    for left in range(4, 0, -1):
        size = (own - start + left - 1) // left
        if size > 0:
            plan.append((start, size))
        start += size
    return plan


def purify_kernel(
    R, C, L, paired, den_hbm, tc_hbm, oc_hbm, out_hbm, col, den, square, low, result,
    den_sem, out_sem, recv, right_sem, left_sem, far_right, far_left, row_sem,
    recv_low, send_low, relay_low, extra, twin_recv, twin_sem, tc, oc,
):
    own = den_hbm.shape[0]
    bs = den_hbm.shape[2]
    kq = oc_hbm.shape[2]
    plan = chunk_plan(own)
    r, c, l = lax.axis_index("row"), lax.axis_index("col"), lax.axis_index("layer")
    g = r * C + c
    partner = l + 1 - 2 * lax.rem(l, 2)
    rows = [lax.rem(r + d, R) for d in range(1, R)]
    odd = lax.rem(l, 2)
    late = range(1, len(plan))
    order = [*late, 0]
    if paired:
        pair, half = l // 4, lax.rem(l // 2, 2)
        twin = l + 2 - 4 * half
        twins = [twin]
        for e in range(1, L // 4):
            first = 4 * lax.rem(pair + e, L // 4) + odd
            twins += [first, first + 2]
    else:
        twins = [lax.rem(l + 2 * d, L) for d in range(1, L // 2)]

    own_copy = pltpu.make_async_copy(den_hbm.at[:, l], col.at[pl.ds(g * own, own)], den_sem.at[0])
    own_copy.start()
    den_copy = pltpu.make_async_copy(den_hbm, den, den_sem.at[1])
    den_copy.start()
    tc_copy = pltpu.make_async_copy(tc_hbm, tc, den_sem.at[3])
    tc_copy.start()
    oc_copy = pltpu.make_async_copy(oc_hbm, oc, den_sem.at[4])
    oc_copy.start()
    if paired:
        twin_copy = pltpu.make_async_copy(
            den_hbm.at[:, twin], extra.at[pl.ds(g * own, own)], den_sem.at[2]
        )
        twin_copy.start()

    barrier = pltpu.get_barrier_semaphore()

    def greet(**where):
        pl.semaphore_signal(barrier, inc=1, device_id=where, device_id_type=MESH)

    for other in rows:
        greet(row=other)
    for other in twins + [partner]:
        greet(layer=other)

    @pl.when(c > 0)
    def _():
        greet(col=c - 1)

    @pl.when(c < C - 1)
    def _():
        greet(col=c + 1)

    inner = jnp.where(c > 0, 1, 0) + jnp.where(c < C - 1, 1, 0)
    pl.semaphore_wait(barrier, (R - 1) + (L // 2) + inner)

    def tiles(group, ch):
        return col.at[pl.ds(group * own + plan[ch][0], plan[ch][1])]

    def move(group, ch, sem, where):
        return pltpu.make_async_remote_copy(
            src_ref=tiles(group, ch),
            dst_ref=tiles(group, ch),
            send_sem=sem,
            recv_sem=recv.at[group, ch],
            device_id=where,
            device_id_type=MESH,
        )

    def arrived(group, ch):
        move(group, ch, den_sem.at[0], {"layer": partner}).wait_recv()

    def to_right(group, ch, sem, act, step=0):
        @pl.when(jnp.minimum(c - step, C - 2 - c) >= 0)
        def _():
            act(move(group, ch, sem, {"col": c + 1}))

    def to_left(group, ch, sem, act, step=0):
        @pl.when(jnp.minimum(C - 1 - step - c, c - 1) >= 0)
        def _():
            act(move(group, ch, sem, {"col": c - 1}))

    def to_rows(group, ch, at, act):
        for d, other in enumerate(rows):
            act(move(group, ch, row_sem.at[d, at, ch], {"row": other}))

    def twin_move(group, ch):
        part = pl.ds(group * own + plan[ch][0], plan[ch][1])
        return pltpu.make_async_remote_copy(
            src_ref=col.at[part],
            dst_ref=extra.at[part],
            send_sem=twin_sem.at[group, ch],
            recv_sem=twin_recv.at[group, ch],
            device_id={"layer": twin},
            device_id_type=MESH,
        )

    def to_twin(group, ch, ok):
        if paired:
            @pl.when(jnp.minimum(ok, -odd) >= 0)
            def _():
                twin_move(group, ch).start()

    def go(copy):
        copy.start()

    def done(copy):
        copy.wait_send()

    own_copy.wait()
    to_rows(g, 0, c, go)
    for ch in order:
        to_right(g, ch, right_sem.at[c, ch], go)
        to_left(g, ch, left_sem.at[c, ch], go)
        if ch > 0:
            to_rows(g, ch, c, go)
    for d, other in enumerate(rows):
        group = other * C + c
        arrived(group, 0)
        to_twin(group, 0, 0)
        to_right(group, 0, far_right.at[d, c], go)
        to_left(group, 0, far_left.at[d, c], go)

    middle = jnp.minimum(jnp.minimum(c, C - 1 - c) - 1, 0)

    def line(step, arrive):
        act = go if arrive else done
        before = jnp.maximum(c - step, 0)
        after = jnp.minimum(c + step, C - 1)
        for ch in order:
            @pl.when(c >= step)
            def _():
                if arrive:
                    arrived(r * C + before, ch)
                if ch > 0:
                    to_rows(r * C + before, ch, before, act)

            to_right(r * C + before, ch, right_sem.at[before, ch], act, step)
            if arrive:
                to_twin(r * C + before, ch, c - step)

            @pl.when(c + step < C)
            def _():
                if arrive:
                    arrived(r * C + after, ch)
                if ch > 0:
                    to_rows(r * C + after, ch, after, act)

            to_left(r * C + after, ch, left_sem.at[after, ch], act, step)
            if arrive:
                to_twin(r * C + after, ch, C - 1 - step - c)
                if ch > 0:
                    crossed(step - 1, [ch], -1 - middle)
        for d, other in enumerate(rows):
            if arrive:
                @pl.when(c >= step)
                def _():
                    arrived(other * C + before, 0)
            to_right(other * C + before, 0, far_right.at[d, before], act, step)
            if arrive:
                to_twin(other * C + before, 0, c - step)
            if arrive:
                @pl.when(c + step < C)
                def _():
                    arrived(other * C + after, 0)
            to_left(other * C + after, 0, far_left.at[d, after], act, step)
            if arrive:
                to_twin(other * C + after, 0, C - 1 - step - c)

    def crossed(step, chunks, ok):
        before = jnp.maximum(c - step, 0)
        after = jnp.minimum(c + step, C - 1)
        left, right = jnp.minimum(c - step, ok), jnp.minimum(C - 1 - step - c, ok)
        for other in rows:
            for ch in chunks:
                @pl.when(left >= 0)
                def _():
                    arrived(other * C + before, ch)

                to_twin(other * C + before, ch, left)
                if step > 0:
                    @pl.when(right >= 0)
                    def _():
                        arrived(other * C + after, ch)

                    to_twin(other * C + after, ch, right)

    for step in range(1, C):
        line(step, True)
        crossed(step - 1, late, middle)
    crossed(C - 1, late, 0)
    den_copy.wait()
    tc_copy.wait()
    oc_copy.wait()

    def masked(ks, wanted, source, layer):
        columns = [[] for _ in range(kq)]
        for k in ks:
            tile = source[k]
            reached = tc[k, layer]
            for q in range(kq):
                columns[q].append(lax.select(reached == wanted[q], tile, jnp.zeros_like(tile)))
        return jnp.concatenate([jnp.concatenate(parts, axis=0) for parts in columns], axis=1)

    def low_move(u, i, sem, where):
        return pltpu.make_async_remote_copy(
            src_ref=low.at[u, i],
            dst_ref=low.at[u, i],
            send_sem=sem,
            recv_sem=recv_low.at[u, i],
            device_id={"layer": where},
            device_id_type=MESH,
        )

    def low_arrived(u, i):
        low_move(u, i, den_sem.at[0], partner).wait_recv()

    def send_row(i, act):
        for d, other in enumerate(twins + [partner]):
            if paired and d == 0:
                @pl.when(odd == 1)
                def _():
                    act(low_move(l, i, send_low.at[0, i], twins[0]))
            else:
                act(low_move(l, i, send_low.at[d, i], other))

    def square_row(i, source, layer):
        wanted = [oc[i, layer, q] for q in range(kq)]
        left = jnp.concatenate([den[i, s] for s in range(L)], axis=1)
        right = masked([tc[g * own + i, s] for s in range(L)], wanted, source, layer)
        total = jnp.dot(left, right, preferred_element_type=jnp.float32)
        low[layer, i] = total.astype(jnp.bfloat16)
        return total

    def own_row(i):
        square[i] = square_row(i, col, l)

    def own_step(i, carry):
        own_row(i)
        send_row(i - 1, go)
        return carry

    own_row(0)
    lax.fori_loop(1, own, own_step, 0)
    send_row(own - 1, go)

    if paired:
        twin_copy.wait()

        @pl.when(odd == 0)
        def _():
            for j in range(1, R * C):
                for ch in order:
                    twin_move(lax.rem(g + j, R * C), ch).wait_recv()

            def pass_on(i):
                low_move(twin, i, relay_low.at[0, i], partner).start()

            def twin_step(i, carry):
                square_row(i, extra, twin)
                pass_on(i - 1)
                return carry

            square_row(0, extra, twin)
            lax.fori_loop(1, own, twin_step, 0)
            pass_on(own - 1)

    def relay(i, act):
        for d, other in enumerate(twins):
            if paired and d == 0 and act is go:
                @pl.when(odd == 1)
                def _():
                    low_arrived(twin, i)
                    low_move(twin, i, relay_low.at[0, i], partner).start()
                continue
            if act is go:
                low_arrived(other, i)
            act(low_move(other, i, relay_low.at[d, i], partner))

    def cube_row(i):
        low_arrived(partner, i)
        for other in twins:
            low_arrived(other + 1 - 2 * lax.rem(other, 2), i)
        wanted = [oc[i, l, q] for q in range(kq)]
        total = jnp.zeros((bs, kq * bs), jnp.float32)
        for u in range(L):
            right = masked([oc[i, u, t] for t in range(kq)], wanted, col, l)
            total += jnp.dot(low[u, i], right, preferred_element_type=jnp.float32)
        value = (3.0 * square[i] - 2.0 * total).astype(jnp.bfloat16)
        for q in range(kq):
            result[i, q] = value[:, q * bs:(q + 1) * bs]

    def write(i):
        return pltpu.make_async_copy(result.at[i], out_hbm.at[i, 0], out_sem.at[i])

    relay(0, go)

    def cube_step(i, carry):
        relay(i, go)
        cube_row(i - 1)

        @pl.when(i > 1)
        def _():
            write(i - 2).start()

        return carry

    lax.fori_loop(1, own, cube_step, 0)
    cube_row(own - 1)
    if own > 1:
        write(own - 2).start()
    write(own - 1).start()

    to_rows(g, 0, c, done)
    for ch in order:
        to_right(g, ch, right_sem.at[c, ch], done)
        to_left(g, ch, left_sem.at[c, ch], done)
        if ch > 0:
            to_rows(g, ch, c, done)
    for d, other in enumerate(rows):
        to_right(other * C + c, 0, far_right.at[d, c], done)
        to_left(other * C + c, 0, far_left.at[d, c], done)
    for step in range(1, C):
        line(step, False)

    if paired:
        @pl.when(odd == 0)
        def _():
            for j in range(1, R * C):
                for ch in order:
                    twin_move(lax.rem(g + j, R * C), ch).wait_send()

    def finish(i, carry):
        send_row(i, done)
        relay(i, done)
        write(i).wait()
        return carry

    lax.fori_loop(0, own, finish, 0)


def on_device(R, C, L, density, tile_cols, out_cols):
    own, _, bs, _ = density.shape
    kq = out_cols.shape[2]
    groups = R * C
    parts = len(chunk_plan(own))
    paired = L % 4 == 0
    dma = pltpu.SemaphoreType.DMA
    bf16, f32 = jnp.bfloat16, jnp.float32
    return pl.pallas_call(
        functools.partial(purify_kernel, R, C, L, paired),
        out_shape=jax.ShapeDtypeStruct((own, 1, kq, bs, bs), bf16),
        in_specs=[
            pl.BlockSpec(memory_space=pl.ANY),
            pl.BlockSpec(memory_space=pl.ANY),
            pl.BlockSpec(memory_space=pl.ANY),
        ],
        out_specs=pl.BlockSpec(memory_space=pl.ANY),
        scratch_shapes=[
            pltpu.VMEM((groups * own, bs, bs), bf16),
            pltpu.VMEM((own, L, bs, bs), bf16),
            pltpu.VMEM((own, bs, kq * bs), f32),
            pltpu.VMEM((L, own, bs, kq * bs), bf16),
            pltpu.VMEM((own, kq, bs, bs), bf16),
            dma((5,)),
            dma((own,)),
            dma((groups, parts)),
            dma((C, parts)),
            dma((C, parts)),
            dma((max(R - 1, 1), C)),
            dma((max(R - 1, 1), C)),
            dma((max(R - 1, 1), C, parts)),
            dma((L, own)),
            dma((L // 2, own)),
            dma((max(L // 2 - 1, 1), own)),
            pltpu.VMEM((groups * own if paired else 1, bs, bs), bf16),
            dma((groups, parts)),
            dma((groups, parts)),
            pltpu.SMEM(tile_cols.shape, jnp.int32),
            pltpu.SMEM(out_cols.shape, jnp.int32),
        ],
        compiler_params=pltpu.CompilerParams(
            collective_id=0, has_side_effects=True, vmem_limit_bytes=60 * 2**20
        ),
    )(density, tile_cols, out_cols)


def solution(mesh):
    R, C, L = (mesh.shape[name] for name in ("row", "col", "layer"))
    placed = (P(("row", "col"), None, None, None), P(), P(("row", "col"), None, None))
    return jax.shard_map(
        functools.partial(on_device, R, C, L),
        mesh=mesh,
        in_specs=placed,
        out_specs=P(("row", "col"), "layer", None, None, None),
        check_vma=False,
    )
```
